768 devices in a mesh: sec: 8 (over z_lo, core), tile: 96 (over x, z_hi, y).
Axes of the slice: x: 4, y: 8, z: 12 (z_hi: 3, z_lo: 4; z = z_hi * 4 + z_lo), core: 2. Of those that a mesh axis runs over, the one named last changes fastest.
Arguments:
- velocity: float32 [3, 192, 192, 128], P(None, 'sec', 'tile'), may hold values from -5 to 8
- prev_tendency: float32 [3, 192, 192, 128], P(None, 'sec', 'tile'), may hold values from -12 to 12
- disk_cells: int32 [8, 96, 256], P('sec', 'tile'), may hold values from 0 to 6144, as said below
- disk_kind: int32 [8, 96, 256], P('sec', 'tile'), may hold values from 0 to 15
- rotor_weights: float32 [16], replicated, may hold values from 0.5 to 2
Outputs:
- velocity_next: float32 [3, 192, 192, 128], P(None, 'sec', 'tile')
- tendency: float32 [3, 192, 192, 128], P(None, 'sec', 'tile')
The draws below stay inside these ranges and needn't reach their ends.
Inputs may be any that keep to these rules, and one draw needn't show every extreme that they name: `disk_cells`: an entry equal to 6144 marks an empty slot; any other entry is a flat index (i * 2 + j) * 128 + k into the device's own block, repeats allowed. Every slot of a device in the first half of the sec indices is empty; some other device has all 256 slots live in every draw.
All inputs are finite; a program needn't handle non-finite values.
Results may differ from the reference program's by a relative error of at most 0.0003.
Values sent between devices are 32-bit elements; how exact they have to be, the bound alone decides.
No kernel may reach another device: no remote copies, remote signals or barrier semaphores. Data moves between devices by JAX's collectives and lax.ppermute only.
A program may use at most 32 MiB of HBM per device.

```python
import math
import jax
import jax.numpy as jnp
from jax import lax

XB = 24
YT = 2
NZ = 128
STEPS = 2
DSLOT = 256
KINDS = 16
NX = 192
NY = 192
N_SEC = 8
N_TILE = 96


def draw_velocity(key, part):
    whole_shape = (3, NX, NY, NZ)
    height = (jnp.arange(NZ).astype(jnp.float32) + 0.5) / NZ
    fluctuation = jnp.clip(jax.random.normal(key, whole_shape, jnp.float32), -5.0, 5.0)
    mean_flow = 1.5 * height[None, None, :] + jnp.zeros((NX, 1, 1), jnp.float32)
    return fluctuation.at[0].add(mean_flow)


def draw_disk_cells(key, part):
    cell_count = XB * YT * NZ
    key_cells, key_live, key_tile, key_sec = jax.random.split(key, 4)
    picked = jax.random.randint(key_cells, (N_SEC, N_TILE, DSLOT), 0, cell_count)
    live_count = jax.random.randint(key_live, (N_SEC, N_TILE), DSLOT // 2, DSLOT + 1)
    full_tile = jax.random.randint(key_tile, (), 0, N_TILE)
    full_sec = jax.random.randint(key_sec, (), N_SEC // 2, N_SEC)
    sec_ids = jnp.arange(N_SEC)[:, None]
    tile_ids = jnp.arange(N_TILE)[None, :]
    live_count = jnp.where((sec_ids == full_sec) & (tile_ids == full_tile), DSLOT, live_count)
    live_count = jnp.where(sec_ids < N_SEC // 2, 0, live_count)
    slot_ids = jnp.arange(DSLOT)[None, None, :]
    return jnp.where(slot_ids < live_count[:, :, None], picked, cell_count).astype(jnp.int32)


def set_ends(entries, rng, low, top_value):
    longest = entries.shape.index(max(entries.shape))
    spots = []
    for shift in (0, 1):
        where = [jax.random.randint(jax.random.fold_in(rng, axis), (), 0, length) for axis, length in enumerate(entries.shape)]
        where[longest] = (where[longest] + shift) % entries.shape[longest]
        spots.append(tuple(where))
    return entries.at[spots[0]].set(low).at[spots[1]].set(top_value)


def block_scale(stream_key, shape, cuts, low, top_value):
    level = 1.0
    for axis_at, parts in cuts:
        steps = jax.random.uniform(jax.random.fold_in(jax.random.fold_in(stream_key, 6), axis_at), (parts,), jnp.float32, low / len(cuts), top_value / len(cuts))
        level = level * jnp.repeat(jnp.exp(steps), shape[axis_at] // parts).reshape((-1,) + (1,) * (len(shape) - 1 - axis_at))
    return level


def noise(stream_key, shape, deviation, reach, cuts=(), held_as=jnp.bfloat16):
    values = jax.random.normal(stream_key, shape, jnp.float32) * deviation
    if len(cuts) > 0:
        values = block_scale(stream_key, shape, cuts, -0.22, 0.18) * values
    return jnp.clip(values, min=-reach, max=reach).astype(held_as)


def setup_inputs(seed: int = 0) -> dict:
    streams_of = jax.random.split(jax.random.key(seed), 6)
    velocity = draw_velocity(jax.random.fold_in(streams_of[5], 71), 0)
    prev_tendency = noise(streams_of[1], (3, NX, NY, NZ), 2.0, 12.0, ((1, 8), (2, 96)), jnp.float32)
    disk_cells = draw_disk_cells(jax.random.fold_in(streams_of[5], 71), 0)
    disk_kind = set_ends(jax.random.randint(streams_of[3], (N_SEC, N_TILE, DSLOT), 0, KINDS), jax.random.fold_in(streams_of[3], 1), 0, KINDS - 1).astype(jnp.int32)
    rotor_weights = jnp.clip(jnp.exp(jax.random.uniform(streams_of[4], (KINDS,), jnp.float32, math.log(0.5), math.log(2.0))), 0.5, 2.0)
    return {"velocity": velocity, "prev_tendency": prev_tendency, "disk_cells": disk_cells, "disk_kind": disk_kind, "rotor_weights": rotor_weights}


precise = lax.Precision.HIGHEST
time_step = 0.1
fringe_rate = 2.0
smag_coef = 0.04

def gradients(padded, z_sign):
    centre = padded[:, 1:-1, 1:-1, :]
    grad_x = 0.5 * (padded[:, 2:, 1:-1, :] - padded[:, :-2, 1:-1, :])
    grad_y = 0.5 * (padded[:, 1:-1, 2:, :] - padded[:, 1:-1, :-2, :])
    extended = jnp.concatenate([z_sign * centre[..., :1], centre, z_sign * centre[..., -1:]], axis=-1)
    grad_z = 0.5 * (extended[..., 2:] - extended[..., :-2])
    return (grad_x, grad_y, grad_z)

def strain_stress(slopes):

    def strain(first, second):
        return 0.5 * (slopes[second][first] + slopes[first][second])
    strain_xx = strain(0, 0)
    strain_yy = strain(1, 1)
    strain_zz = strain(2, 2)
    strain_xy = strain(0, 1)
    strain_xz = strain(0, 2)
    strain_yz = strain(1, 2)
    squared = strain_xx * strain_xx + strain_yy * strain_yy + strain_zz * strain_zz
    squared = squared + 2.0 * (strain_xy * strain_xy + strain_xz * strain_xz + strain_yz * strain_yz)
    double = 2.0 * (smag_coef * jnp.sqrt(2.0 * squared + 0.01))
    return jnp.stack([double * strain_xx, double * strain_yy, double * strain_zz, double * strain_xy, double * strain_xz, double * strain_yz])

def advection(slopes, centre):
    return centre[0:1] * slopes[0] + centre[1:2] * slopes[1] + centre[2:3] * slopes[2]

def stress_force(padded):
    grad_x, grad_y, grad_z = gradients(padded, 0.0)
    return jnp.stack([grad_x[0] + grad_y[3] + grad_z[4], grad_x[3] + grad_y[1] + grad_z[5], grad_x[4] + grad_y[5] + grad_z[2]])

def wrap_pad(source):
    return jnp.pad(source, ((0, 0), (1, 1), (1, 1), (0, 0)), mode='wrap')

def hartley(source, axis):
    spectrum = jnp.fft.fft(source, axis=axis)
    return spectrum.real - spectrum.imag

def cosine_table():
    modes = jnp.arange(NZ).astype(jnp.float32)[:, None]
    points = jnp.arange(NZ).astype(jnp.float32)[None, :] + 0.5
    return jnp.cos(math.pi * modes * points / NZ)

def spectral_inverse():
    mode_x = jnp.arange(NX)
    mode_y = jnp.arange(NY)
    mode_z = jnp.arange(NZ)
    sin_x = jnp.sin(2.0 * math.pi * mode_x.astype(jnp.float32) / NX)
    sin_y = jnp.sin(2.0 * math.pi * mode_y.astype(jnp.float32) / NY)
    sin_z = jnp.sin(math.pi * mode_z.astype(jnp.float32) / NZ)
    eigen = -((sin_x * sin_x)[:, None, None] + (sin_y * sin_y)[None, :, None] + (sin_z * sin_z)[None, None, :])
    zero_mode = (mode_x % (NX // 2) == 0)[:, None, None] & (mode_y % (NY // 2) == 0)[None, :, None] & (mode_z == 0)[None, None, :]
    return jnp.where(zero_mode, 0.0, 1.0 / jnp.where(zero_mode, 1.0, eigen))

def solve_pressure(rhs, cos_tab, weights, recip):
    coeffs = jnp.einsum('xyz,mz->xym', rhs, cos_tab, precision=precise)
    coeffs = hartley(hartley(coeffs, 0), 1)
    coeffs = coeffs * recip
    coeffs = hartley(hartley(coeffs, 1), 0) / (NX * NY)
    return jnp.einsum('xym,mz->xyz', coeffs * weights[None, None, :], cos_tab, precision=precise)

def turbine_push(axial, disk_cells, disk_kind, rotor_weights):
    cell_count = XB * YT * NZ
    blocks = axial.reshape(N_SEC, XB, N_TILE, YT, NZ).transpose(0, 2, 1, 3, 4).reshape(N_SEC * N_TILE, cell_count)
    picked = disk_cells.reshape(N_SEC * N_TILE, DSLOT)
    kinds = disk_kind.reshape(N_SEC * N_TILE, DSLOT)
    live = picked < cell_count
    safe = jnp.minimum(picked, cell_count - 1).astype(jnp.int32)
    sampled = jnp.take_along_axis(blocks, safe, axis=1)
    weight = rotor_weights[kinds]
    push = jnp.where(live, -(weight * sampled * jnp.abs(sampled)), 0.0)
    row_ids = jnp.arange(N_SEC * N_TILE).astype(jnp.int32)[:, None]
    summed = jnp.zeros_like(blocks).at[row_ids, safe].add(push)
    return summed.reshape(N_SEC, N_TILE, XB, YT, NZ).transpose(0, 2, 1, 3, 4).reshape(NX, NY, NZ)

def reference(velocity, prev_tendency, disk_cells, disk_kind, rotor_weights):
    cos_tab = cosine_table()
    weights = jnp.where(jnp.arange(NZ) == 0, 1.0 / NZ, 2.0 / NZ).astype(jnp.float32)
    recip = spectral_inverse()
    root_slab = N_SEC // 2 - 1
    slab_pos = jnp.sin(math.pi * (jnp.arange(XB).astype(jnp.float32) + 0.5) / XB)
    lam_x = fringe_rate * (slab_pos * slab_pos)
    sec_ids = jnp.arange(N_SEC)
    flags = ((sec_ids == 0) | (sec_ids == N_SEC // 2) | (sec_ids == 3 * N_SEC // 4) | (sec_ids == N_SEC - 1)).astype(jnp.float32)
    current = velocity
    tendency_old = prev_tendency
    tendency = prev_tendency
    for step_no in range(STEPS):
        slopes = gradients(wrap_pad(current), -1.0)
        stress = strain_stress(slopes)
        advect = advection(slopes, current)
        push_field = stress_force(wrap_pad(stress))
        blocks = current.reshape(3, N_SEC, XB, NY, NZ)
        target = blocks[:, root_slab]
        fringe = flags[None, :, None, None, None] * lam_x[None, None, :, None, None] * (target[:, None] - blocks)
        fringe = fringe.reshape(current.shape)
        turbine = turbine_push(current[0], disk_cells, disk_kind, rotor_weights)
        empty = jnp.zeros_like(turbine)
        tendency = push_field - advect + jnp.stack([turbine, empty, empty]) + fringe
        interim = current + time_step * (1.5 * tendency - 0.5 * tendency_old)
        grad_x, grad_y, grad_z = gradients(wrap_pad(interim), -1.0)
        rhs = grad_x[0] + grad_y[1] + grad_z[2]
        pressure = solve_pressure(rhs, cos_tab, weights, recip)
        press_x, press_y, press_z = gradients(wrap_pad(pressure[None]), 1.0)
        current = interim - jnp.concatenate([press_x, press_y, press_z], axis=0)
        tendency_old = tendency
    return (current, tendency)
```

```python
import math

import jax
import jax.numpy as jnp
import numpy as np
from jax import lax
from jax.sharding import Mesh
from jax.sharding import PartitionSpec as P

STEPS = 2
KINDS = 16

precise = lax.Precision.HIGHEST
time_step = 0.1
fringe_rate = 2.0
smag_coef = 0.04

TILE = ("tx", "tz", "ty")
NEAR = ("sec", "tx")
FAR = ("tz", "ty")
SPLITS = {96: (4, 3, 8), 4: (2, 1, 2)}


def gradients(padded, z_sign):
    centre = padded[:, 1:-1, 1:-1, :]
    grad_x = 0.5 * (padded[:, 2:, 1:-1, :] - padded[:, :-2, 1:-1, :])
    grad_y = 0.5 * (padded[:, 1:-1, 2:, :] - padded[:, 1:-1, :-2, :])
    extended = jnp.concatenate(
        [z_sign * centre[..., :1], centre, z_sign * centre[..., -1:]], axis=-1
    )
    grad_z = 0.5 * (extended[..., 2:] - extended[..., :-2])
    return (grad_x, grad_y, grad_z)


def strain_stress(slopes):

    def strain(first, second):
        return 0.5 * (slopes[second][first] + slopes[first][second])

    strain_xx = strain(0, 0)
    strain_yy = strain(1, 1)
    strain_zz = strain(2, 2)
    strain_xy = strain(0, 1)
    strain_xz = strain(0, 2)
    strain_yz = strain(1, 2)
    squared = strain_xx * strain_xx + strain_yy * strain_yy + strain_zz * strain_zz
    squared = squared + 2.0 * (
        strain_xy * strain_xy + strain_xz * strain_xz + strain_yz * strain_yz
    )
    double = 2.0 * (smag_coef * jnp.sqrt(2.0 * squared + 0.01))
    return jnp.stack(
        [
            double * strain_xx,
            double * strain_yy,
            double * strain_zz,
            double * strain_xy,
            double * strain_xz,
            double * strain_yz,
        ]
    )


def stress_force(padded):
    grad_x, grad_y, grad_z = gradients(padded, 0.0)
    return jnp.stack(
        [
            grad_x[0] + grad_y[3] + grad_z[4],
            grad_x[3] + grad_y[1] + grad_z[5],
            grad_x[4] + grad_y[5] + grad_z[2],
        ]
    )


def ring(count, shift):
    return [(i, (i + shift) % count) for i in range(count)]


def cas(rows, cols, length):
    angle = 2.0 * np.pi * ((np.asarray(rows)[:, None] * np.asarray(cols)[None, :]) % length)
    angle = angle / length
    return np.cos(angle) + np.sin(angle)


def wave_sin(count, length):
    values = np.sin(np.pi * np.arange(count) / length) ** 2
    values[np.arange(count) % length == 0] = 0.0
    return values.astype(np.float32)


def make_tables(n_sec, split, slab, wide, depth):
    tx, tz, ty = split
    far = tz * ty
    full_x, full_y = slab * n_sec, wide * tx * far
    part_x = full_x // far
    part_z = depth // (n_sec * tx)
    points = np.arange(depth) + 0.5
    cosine = np.cos(np.pi * np.arange(depth)[:, None] * points[None, :] / depth)
    slope = 0.5 * (np.eye(depth, k=1) - np.eye(depth, k=-1))
    slope[0, 0] = 0.5
    slope[-1, -1] = -0.5
    forward_z = np.stack([cosine, cosine, cosine @ slope])

    def forward(length):
        plain = cas(np.arange(length), np.arange(length), length)
        return plain, 0.5 * (np.roll(plain, 1, axis=1) - np.roll(plain, -1, axis=1))

    plain_x, slope_x = forward(full_x)
    zero = np.zeros_like(plain_x)
    forward_x = np.stack(
        [np.stack([slope_x, zero, plain_x]), np.stack([zero, plain_x, zero])]
    )
    forward_x = forward_x.reshape(2, 3, full_x, n_sec, slab).transpose(0, 2, 3, 1, 4)
    plain_y, slope_y = forward(full_y)
    forward_y = np.stack([plain_y, slope_y]).reshape(2, full_y, tx, far, wide)
    forward_y = forward_y.transpose(1, 3, 0, 2, 4)

    def back_y(halo):
        inner = np.arange(wide + 2 * halo) - halo
        rows = (
            (np.arange(tx) * far * wide)[None, :, None]
            + (np.arange(far) * wide)[:, None, None]
            + inner
        ) % full_y
        table = cas(rows.reshape(-1), np.arange(full_y), full_y)
        return table.reshape(far, tx, wide + 2 * halo, full_y)

    def back_x(halo):
        inner = np.arange(slab + 2 * halo) - halo
        rows = ((np.arange(n_sec) * slab)[:, None] + inner) % full_x
        table = cas(rows.reshape(-1), np.arange(full_x), full_x)
        return table.reshape(n_sec, slab + 2 * halo, far, part_x)

    weight = np.full(depth, 2.0 / depth)
    weight[0] = 1.0 / depth
    weight = weight / (full_x * full_y)
    return dict(
        forward_z=forward_z,
        forward_x=forward_x,
        forward_y=forward_y,
        back_y=back_y,
        back_x=back_x,
        cosine=cosine,
        weight=weight,
        sin_x=wave_sin(full_x, full_x // 2),
        sin_y=wave_sin(full_y, full_y // 2),
        sin_z=wave_sin(depth, depth),
        part_x=part_x,
        part_z=part_z,
    )


def f32(table):
    return jnp.asarray(np.asarray(table, np.float32))


def pressure_slopes(pressure):
    grads = gradients(pressure[None], 1.0)
    return jnp.concatenate(grads, axis=0)


def local(n_sec, split, velocity, prev_tendency, disk_cells, disk_kind, rotor_weights):
    slab, wide, depth = velocity.shape[1:]
    tx, tz, ty = split
    far, near, tiles = tz * ty, n_sec * tx, tx * tz * ty
    tab = make_tables(n_sec, split, slab, wide, depth)
    part_x, part_z = tab["part_x"], tab["part_z"]
    sec_at = lax.axis_index("sec")
    near_at = lax.axis_index(NEAR)
    far_at = lax.axis_index(FAR)
    root = n_sec // 2 - 1
    fringe_slabs = (0, n_sec // 2, 3 * n_sec // 4, n_sec - 1)

    def with_halo(field):
        low = lax.ppermute(field[:, -2:], "sec", ring(n_sec, 1))
        high = lax.ppermute(field[:, :2], "sec", ring(n_sec, -1))
        field = jnp.concatenate([low, field, high], axis=1)
        low = lax.ppermute(field, TILE, ring(tiles, 1))
        high = lax.ppermute(field, TILE, ring(tiles, -1))
        return jnp.concatenate([low, field, high], axis=2)

    def from_root(field):
        total = None
        for target in fringe_slabs:
            got = lax.ppermute(field, "sec", [(root, target)])
            total = got if total is None else total + got
        return total

    lam = fringe_rate * np.sin(np.pi * (np.arange(slab) + 0.5) / slab) ** 2
    flag = jnp.zeros((), jnp.float32)
    for target in fringe_slabs:
        flag = flag + (sec_at == target).astype(jnp.float32)
    lam_x = flag * f32(lam)[None, :, None, None]

    rows = slab * wide
    picked = disk_cells.reshape(-1)
    kinds = disk_kind.reshape(-1)
    weight = jnp.sum(
        jnp.where(kinds[:, None] == jnp.arange(KINDS)[None, :], rotor_weights[None, :], 0.0), axis=1
    )
    at_row = (picked // depth)[None, :] == jnp.arange(rows)[:, None]
    at_lane = (picked % depth)[:, None] == jnp.arange(depth)[None, :]
    drag = jnp.dot(
        jnp.where(at_row, weight[None, :], 0.0),
        at_lane.astype(jnp.float32),
        precision=precise,
    ).reshape(slab, wide, depth)

    wave_x = lax.dynamic_slice_in_dim(jnp.asarray(tab["sin_x"]), far_at * part_x, part_x)
    wave_z = lax.dynamic_slice_in_dim(jnp.asarray(tab["sin_z"]), near_at * part_z, part_z)
    wave_w = lax.dynamic_slice_in_dim(f32(tab["weight"]), near_at * part_z, part_z)
    wave_y = jnp.asarray(tab["sin_y"])
    eigen = wave_y[:, None, None] + wave_x[None, :, None] + wave_z[None, None, :]
    recip = jnp.where(eigen == 0.0, 0.0, -wave_w / jnp.where(eigen == 0.0, 1.0, eigen))

    def exchange(blocks, axes):
        return lax.all_to_all(blocks, axes, split_axis=0, concat_axis=0, tiled=True)

    def solve(interim, halo, with_root):
        long, broad = slab + 2 * halo, wide + 2 * halo
        coeffs = jnp.einsum("fxyz,fmz->fxym", interim, f32(tab["forward_z"]), precision=precise)
        coeffs = coeffs.reshape(3, slab, wide, near, part_z).transpose(3, 0, 1, 2, 4)
        got = exchange(coeffs.reshape(near, -1), NEAR)
        got = got.reshape(n_sec, tx, 3, slab, wide, part_z)
        along_x = jnp.einsum("gKsfx,safxjk->gKajk", f32(tab["forward_x"]), got, precision=precise)
        along_x = along_x.reshape(2, far, part_x, tx, wide, part_z).transpose(1, 0, 3, 4, 2, 5)
        got = exchange(along_x.reshape(far, -1), FAR)
        got = got.reshape(far, 2, tx, wide, part_x, part_z)
        scaled = recip * jnp.einsum(
            "lqgaj,qgajxk->lxk", f32(tab["forward_y"]), got, precision=precise
        )
        back = jnp.einsum("qayl,lxk->qayxk", f32(tab["back_y"](halo)), scaled, precision=precise)
        got = exchange(back.reshape(far, -1), FAR)
        got = got.reshape(far, tx, broad, part_x, part_z)
        back = jnp.einsum("sxqK,qayKk->sakxy", f32(tab["back_x"](halo)), got, precision=precise)
        pieces = back.reshape(near, part_z, long * broad)
        if with_root:
            trim = slice(halo - 1, 1 - halo)
            source = back[root][:, :, trim, trim].reshape(1, tx, part_z, -1)
            source = jnp.broadcast_to(source, (n_sec,) + source.shape[1:])
            pieces = jnp.concatenate([pieces, source.reshape(near, part_z, -1)], axis=2)
        cells = pieces.shape[2]
        got = exchange(pieces.reshape(near, -1), NEAR).reshape(depth, cells)
        pressure = jnp.einsum("mn,mz->nz", got, f32(tab["cosine"]), precision=precise)
        own = pressure[: long * broad].reshape(long, broad, depth)
        if with_root:
            return own, pressure[long * broad :].reshape(slab + 2, wide + 2, depth)
        return own

    source = from_root(velocity)
    extended = with_halo(velocity)
    tendency_old = prev_tendency
    for step_no in range(STEPS):
        current = extended[:, 2:-2, 2:-2]
        slopes = gradients(extended, -1.0)
        push = stress_force(strain_stress(slopes))
        inner = [slope[:, 1:-1, 1:-1] for slope in slopes]
        advect = current[0:1] * inner[0] + current[1:2] * inner[1] + current[2:3] * inner[2]
        fringe = lam_x * (source - current)
        turbine = -(drag * current[0] * jnp.abs(current[0]))
        tendency = push - advect + fringe
        tendency = tendency.at[0].add(turbine)
        interim = current + time_step * (1.5 * tendency - 0.5 * tendency_old)
        tendency_old = tendency
        if step_no < STEPS - 1:
            source = from_root(interim)
            extended = with_halo(interim)
            pressure, root_pressure = solve(interim, 3, True)
            extended = extended - pressure_slopes(pressure)
            source = source - pressure_slopes(root_pressure)
        else:
            pressure = solve(interim, 1, False)
            current = interim - pressure_slopes(pressure)
    return (current, tendency)


def solution(mesh):
    n_sec, tiles = mesh.shape["sec"], mesh.shape["tile"]
    split = SPLITS[tiles]
    fine = Mesh(mesh.devices.reshape((n_sec,) + split), ("sec",) + TILE)
    blocks = P(None, "sec", TILE, None)
    slots = P("sec", TILE, None)

    def body(*args):
        return local(n_sec, split, *args)

    return jax.shard_map(
        body,
        mesh=fine,
        in_specs=(blocks, blocks, slots, slots, P()),
        out_specs=(blocks, blocks),
        check_vma=False,
    )
```

```python
import functools
import math

import jax
import jax.numpy as jnp
import numpy as np
from jax import lax
from jax.experimental import pallas as pl
from jax.experimental.pallas import tpu as pltpu
from jax.sharding import Mesh
from jax.sharding import PartitionSpec as P

STEPS = 2
KINDS = 16
INTERPRET = False

precise = lax.Precision.HIGHEST
time_step = 0.1
fringe_rate = 2.0
smag_coef = 0.04

TILE = ("tx", "tz", "ty")
NEAR = ("sec", "ty")
FAR = ("tx", "tz")
SPLITS = {96: (4, 3, 8), 24: (1, 3, 8), 16: (2, 1, 8)}
WIDE = 256
SPAN = 24
TOP = 8


def gradients(padded, z_sign):
    centre = padded[:, 1:-1, 1:-1, :]
    grad_x = 0.5 * (padded[:, 1:-1, 2:, :] - padded[:, 1:-1, :-2, :])
    grad_y = 0.5 * (padded[:, 2:, 1:-1, :] - padded[:, :-2, 1:-1, :])
    extended = jnp.concatenate(
        [z_sign * centre[..., :1], centre, z_sign * centre[..., -1:]], axis=-1
    )
    grad_z = 0.5 * (extended[..., 2:] - extended[..., :-2])
    return (grad_x, grad_y, grad_z)


def strain_stress(slopes):

    def strain(first, second):
        return 0.5 * (slopes[second][first] + slopes[first][second])

    strain_xx = strain(0, 0)
    strain_yy = strain(1, 1)
    strain_zz = strain(2, 2)
    strain_xy = strain(0, 1)
    strain_xz = strain(0, 2)
    strain_yz = strain(1, 2)
    squared = strain_xx * strain_xx + strain_yy * strain_yy + strain_zz * strain_zz
    squared = squared + 2.0 * (
        strain_xy * strain_xy + strain_xz * strain_xz + strain_yz * strain_yz
    )
    double = 2.0 * (smag_coef * jnp.sqrt(2.0 * squared + 0.01))
    return jnp.stack(
        [
            double * strain_xx,
            double * strain_yy,
            double * strain_zz,
            double * strain_xy,
            double * strain_xz,
            double * strain_yz,
        ]
    )


def stress_force(padded):
    grad_x, grad_y, grad_z = gradients(padded, 0.0)
    return jnp.stack(
        [
            grad_x[0] + grad_y[3] + grad_z[4],
            grad_x[3] + grad_y[1] + grad_z[5],
            grad_x[4] + grad_y[5] + grad_z[2],
        ]
    )


def ring(count, shift):
    return [(i, (i + shift) % count) for i in range(count)]


def f32(table):
    return jnp.asarray(np.asarray(table, np.float32))


def cas(rows, cols, length):
    angle = 2.0 * np.pi * ((np.asarray(rows)[:, None] * np.asarray(cols)[None, :]) % length)
    angle = angle / length
    return np.cos(angle) + np.sin(angle)


def lane_modes(full_x):
    modes = np.zeros(WIDE, np.int64)
    modes[:full_x] = np.arange(full_x)
    modes[full_x + 1] = full_x // 2
    return modes


def z_tables(depth, near):
    points = np.arange(depth) + 0.5
    modes = np.arange(depth)
    cosine = np.cos(np.pi * modes[:, None] * points[None, :] / depth)
    sine = np.sin(np.pi * modes[:, None] * points[None, :] / depth)
    sine[0] = (-1.0) ** np.arange(depth)
    weight = np.where(modes == 0, 1.0 / depth, 2.0 / depth)[:, None]
    part = depth // near

    def order(table):
        return f32(table.reshape(near, part, depth).transpose(1, 0, 2).reshape(depth, depth))

    return order(cosine), order(sine), order(cosine * weight), order(sine * weight)


def x_tables(n_sec, slab):
    full_x = n_sec * slab
    modes = lane_modes(full_x)
    plain = cas(np.arange(full_x), modes, full_x)
    plain[:, full_x + 2 :] = 0.0
    slope = 0.5 * (np.roll(plain, -1, axis=0) - np.roll(plain, 1, axis=0))

    def pad_x(table):
        table = table.reshape(n_sec, slab, WIDE)
        return f32(np.pad(table, ((0, 0), (0, 32 - slab), (0, 0))).reshape(WIDE, WIDE))

    def back(halo):
        inner = np.arange(32) - halo
        at = (np.arange(n_sec) * slab)[:, None] + inner
        table = np.zeros((WIDE, WIDE))
        table[:full_x] = cas(np.arange(full_x), at.reshape(-1) % full_x, full_x) / full_x
        ahead = cas(np.arange(full_x), (at.reshape(-1) + 1) % full_x, full_x)
        behind = cas(np.arange(full_x), (at.reshape(-1) - 1) % full_x, full_x)
        grad = np.zeros((WIDE, WIDE))
        grad[:full_x] = 0.5 * (ahead - behind) / full_x
        return f32(table), f32(grad)

    return pad_x(plain), pad_x(-slope), back


def line_tables(n_sec, slab, depth, size, blocks, near_at, far_at):
    full_x = n_sec * slab
    count = size * blocks
    near = n_sec * size
    part = depth // near
    modes = lane_modes(full_x)
    wave_x = np.sin(2.0 * np.pi * modes / full_x) ** 2
    wave_x[modes % (full_x // 2) == 0] = 0.0
    wave_z = np.sin(np.pi * np.arange(depth) / depth) ** 2
    both = wave_z[:, None] + wave_x[None, :]
    rate = 2.0 * np.arcsinh(np.sqrt(both))
    safe = np.where(rate == 0.0, 1.0, rate)
    scale = np.where(rate == 0.0, 0.0, 2.0 / (np.sinh(safe) * (1.0 - np.exp(-count * safe))))
    flat = rate == 0.0
    twin = flat & (np.arange(WIDE) >= full_x)[None, :]

    def mine(table):
        return lax.dynamic_slice_in_dim(f32(table), near_at * part, part)

    mu, gain = mine(rate), mine(scale)
    flat, twin = mine(flat) > 0.5, mine(twin) > 0.5

    def decay(distance):
        return jnp.exp(-distance * mu_of(distance))

    def mu_of(distance):
        return mu.reshape((part,) + (1,) * (distance.ndim - 2) + (WIDE,))

    def lanes(table, like):
        return table.reshape((part,) + (1,) * (like.ndim - 2) + (WIDE,))

    def grid(values):
        values = jnp.asarray(values, jnp.float32)
        return jnp.broadcast_to(values[None, ..., None], (part,) + values.shape + (1,))

    def pick(plain, special, like):
        return jnp.where(lanes(flat, like), special, plain)

    index = grid(np.arange(-1, size + 1))
    second = jnp.where(lanes(twin, index), index * index, jnp.ones_like(index))
    first_w = pick(decay(index), second, index)
    second_w = pick(decay(size - 1 - index), index, index)
    second_w = jnp.where(lanes(twin, index), 0.0, second_w)

    def green(distance):
        plain = -lanes(gain, distance) * (decay(distance) + decay(count - distance))
        special = 2.0 * distance * (count - distance) / count - (count**2 - 1) / (3.0 * count)
        return pick(plain, special, distance)

    cells = np.arange(SPAN) - TOP
    valid = ((cells >= -2) & (cells <= size + 1)).astype(np.float32)
    keep = grid(valid)
    sources = np.concatenate([np.arange(size), [-1, size]])
    direct = green(grid(np.abs(cells[None, :] - sources[:, None]))) * keep[:, None]
    spot = grid(cells)
    from_low = pick(-lanes(gain, spot) * decay(spot), 1.0, spot) * keep
    from_high = pick(-lanes(gain, spot) * decay(size - 1 - spot), spot, spot) * keep
    square = pick(0.0, -2.0 * spot * spot / count, spot) * keep
    shift = pick(0.0, -2.0 / count + 0.0 * spot, spot) * keep

    step = lax.rem(far_at - jnp.arange(blocks) + blocks, blocks).astype(jnp.float32)
    away = jnp.broadcast_to(step[None, :, None], (part, blocks, 1))
    other = away > 0.5
    jump = size * away
    low_two = pick(decay(jump - (size - 1)), 2.0 * (2.0 * jump - count) / count, jump)
    low_one = pick(
        0.0,
        2.0 * jump * (count - jump) / count - (count**2 - 1) / (3.0 * count),
        jump,
    )
    high_one = pick(decay(count - (size - 1) - jump), 2.0 * (count - 2.0 * jump) / count, jump)
    high_two = pick(0.0, 4.0 / count + 0.0 * jump, jump)
    whole = jnp.ones_like(low_two)

    def rows(one, two):
        pair = jnp.stack([jnp.broadcast_to(one, low_two.shape), jnp.broadcast_to(two, low_two.shape)], 2)
        pair = jnp.where(other[..., None], pair, 0.0)
        pair = jnp.broadcast_to(pair[:, :, None], (part, blocks, 2, 2, WIDE))
        return pair.transpose(1, 0, 2, 3, 4).reshape(blocks, part * 4, WIDE)

    combine = jnp.stack([rows(low_one, low_two), rows(high_one, high_two), rows(whole, 0.0 * whole)])
    spread = jnp.stack([from_low, from_high, square, shift])
    wave = mine(np.broadcast_to(np.sin(np.pi * np.arange(depth) / depth)[:, None], (depth, WIDE)))
    return dict(first=first_w, second=second_w, direct=direct, spread=spread, combine=combine, wave=wave)


def dot(left, right, contract):
    return lax.dot_general(
        left, right, (contract, ((), ())), precision=precise, preferred_element_type=jnp.float32
    )


def kernel(body, out_shapes, scratch, *operands, scalars=0):
    spaces = [pl.BlockSpec(memory_space=pltpu.SMEM)] * scalars
    spaces += [pl.BlockSpec(memory_space=pltpu.VMEM)] * (len(operands) - scalars)
    shapes = [jax.ShapeDtypeStruct(shape, jnp.float32) for shape in out_shapes]
    moved = sum(4 * math.prod(item.shape) for item in list(operands) + shapes)
    return pl.pallas_call(
        body,
        out_shape=shapes,
        in_specs=spaces,
        out_specs=[pl.BlockSpec(memory_space=pltpu.VMEM)] * len(shapes),
        scratch_shapes=[pltpu.VMEM(shape, jnp.float32) for shape in scratch],
        cost_estimate=pl.CostEstimate(flops=10**7, bytes_accessed=moved, transcendentals=0),
        compiler_params=pltpu.CompilerParams(vmem_limit_bytes=24 * 2**20),
        interpret=pltpu.InterpretParams() if INTERPRET else False,
    )(*operands)


def forward_z(near, slab, part, field, cos_rows, sin_rows, out, even, odd):
    even[...] = jnp.zeros_like(even)
    odd[...] = jnp.zeros_like(odd)
    for j in range(2):
        for c in range(3):
            kept = even if c < 2 else odd
            kept[j * 128 + c * 32 : j * 128 + c * 32 + slab, :] = field[c, j]
    result = dot(cos_rows[...], even[...], ((1,), (1,)))
    result = result + dot(sin_rows[...], odd[...], ((1,), (1,)))
    for k in range(part):
        for j in range(2):
            piece = result[k * near : (k + 1) * near, j * 128 : (j + 1) * 128]
            out[pl.ds(k * 2 + j, near, stride=2 * part), :] = piece


def slot_of(shape):
    return lax.broadcasted_iota(jnp.int32, shape, 1) // 32


def moved_to(piece, source, target):
    shift = (32 * (target - source)) % 128
    return piece if shift == 0 else pltpu.roll(piece, shift, 1)


def forward_x(
    part, edges, blocks, got, plain, slope, first, second, wave, out, modes, inner, ends, lhs, rows
):
    slots = slot_of((8, 128))
    groups = 2 * part
    for t in range(2):
        for g in range(groups):
            for c in range(3):
                total = None
                for u in range(4):
                    s = 4 * t + u
                    piece = got[pl.ds(s * 8 * groups + g, 8, stride=groups), :]
                    piece = moved_to(piece, c, u)
                    total = piece if total is None else jnp.where(slots == u, piece, total)
                base = c * 8 * groups + g * 8
                lhs[base : base + 8, t * 128 : (t + 1) * 128] = total
    height = 8 * groups
    fields = dot(lhs[...], plain[...], ((1,), (0,)))
    modes[...] = fields
    sloped = dot(lhs[0:height, :], slope[...], ((1,), (0,)))
    at_row = lax.broadcasted_iota(jnp.int32, (8, WIDE), 0)
    for k in range(part):
        sources = []
        crossing = []
        for j in range(2):
            base = (2 * k + j) * 8
            vertical = modes[2 * height + base : 2 * height + base + 8, :]
            sources.append(sloped[base : base + 8] + wave[k : k + 1, :] * vertical)
            crossing.append(modes[height + base : height + base + 8, :])
        below = jnp.where(at_row == 0, 0.0, pltpu.roll(crossing[1], 1, 0))
        above = jnp.where(at_row == 7, 0.0, pltpu.roll(crossing[0], 7, 0))
        lines = [
            sources[0] + 0.5 * (crossing[1] - below),
            sources[1] + 0.5 * (above - crossing[0]),
        ]
        outside = [-0.5 * crossing[1][7:8, :], 0.5 * crossing[0][0:1, :]]
        for j in range(2):
            base = (2 * k + j) * 8
            inner[base : base + 8, :] = lines[j]
            ends[2 * k + j : 2 * k + j + 1, :] = outside[j]
            past = 9 if j == 0 else 0
            for r, table in enumerate((first, second)):
                moment = jnp.sum(table[k, 1:9, :] * lines[j], axis=0, keepdims=True)
                moment = moment + table[k, past : past + 1, :] * outside[j]
                at = k * 4 + j * 2 + r
                rows[at : at + 1, :] = moment
    if edges:
        for k in range(part):
            for c in range(3):
                for e in range(4):
                    source = c * height + (2 * k + e % 2) * 8 + (0 if e < 2 else 7)
                    at = 4 * part + k * 12 + c * 4 + e
                    rows[at : at + 1, :] = modes[source : source + 1, :]
    size = rows.shape[0]
    for h in range(2):
        half = rows[:, h * 128 : (h + 1) * 128]
        for n in range(blocks):
            out[(n * 2 + h) * size : (n * 2 + h + 1) * size, :] = half


def back_x(
    part, edges, blocks, full_x, root, *refs
):
    if edges:
        (sides, got, modes, inner, ends, direct, spread, combine, wave, back, grad, out, work) = refs
    else:
        (got, inner, ends, direct, spread, combine, back, out, work) = refs
    size = got.shape[0] // (2 * blocks)
    groups = 2 * part
    height = 8 * groups
    lane = lax.broadcasted_iota(jnp.int32, (1, WIDE), 1)
    sums = []
    for r in range(3):
        halves = []
        for h in range(2):
            total = None
            for n in range(blocks):
                piece = got[(n * 2 + h) * size : (n * 2 + h) * size + 4 * part, :]
                piece = combine[r, n, :, h * 128 : (h + 1) * 128] * piece
                total = piece if total is None else total + piece
            halves.append(total)
        sums.append(jnp.concatenate(halves, axis=1))
    side_rows = []
    if edges:
        for which in range(2):
            halves = []
            for h in range(2):
                start = pl.multiple_of((sides[which] * 2 + h) * size + 4 * part, 8)
                halves.append(got[pl.ds(start, 12 * part), :])
            side_rows.append(jnp.concatenate(halves, axis=1))

    def side(which, k, c, e):
        at = k * 12 + c * 4 + e
        return side_rows[which][at : at + 1, :]

    at_row = lax.broadcasted_iota(jnp.int32, (SPAN, WIDE), 0)
    row8 = lax.broadcasted_iota(jnp.int32, (8, WIDE), 0)
    pressure = []
    for k in range(part):
        for j in range(2):
            g = 2 * k + j
            line = inner[g * 8 : g * 8 + 8, :]
            total = None
            for i in range(8):
                term = direct[k, i] * line[i : i + 1, :]
                total = term if total is None else total + term
            total = total + direct[k, 9 if j == 0 else 8] * ends[g : g + 1, :]
            for r in range(3):
                one = sums[r][2 * g : 2 * g + 1, :] + sums[r][2 * g + 1 : 2 * g + 2, :]
                total = total + spread[r, k] * one
                if r == 2:
                    far = jnp.where(
                        lane == 0,
                        one[:, full_x : full_x + 1],
                        jnp.where(lane == full_x // 2, one[:, full_x + 1 : full_x + 2], 0.0),
                    )
                    total = total + spread[3, k] * far
            pressure.append(total)
    if edges:
        wrap = []
        for c in range(3):
            for k in range(part):
                for j in range(2):
                    g = 2 * k + j
                    own = modes[c * height + g * 8 : c * height + g * 8 + 8, :]
                    low = jnp.where(row8 == 7, side(0, k, c, 2 + j), 0.0)
                    high = jnp.where(row8 == 0, side(1, k, c, j), 0.0)
                    wrap.append(jnp.concatenate([low, own, high], axis=0))
        return wrap_up(part, full_x, root, wrap, pressure, side, at_row, wave, back, grad, out, work)
    work[...] = dot(jnp.concatenate(pressure, axis=0), back[...], ((1,), (0,)))
    slots = slot_of((8, 128))
    picks = ((1, -1), (0, 0), (1, 0), (0, 1))
    for s in range(8):
        for k in range(part):
            tile = None
            for v, (j, off) in enumerate(picks):
                base = (2 * k + j) * SPAN + TOP + off
                piece = work[base : base + 8, (s // 4) * 128 : (s // 4) * 128 + 128]
                piece = moved_to(piece, s % 4, v)
                tile = piece if tile is None else jnp.where(slots == v, piece, tile)
            out[pl.ds(s * 8 * part + k, 8, stride=part), :] = tile


def slots_back():
    first = [(c, y, False) for c in range(2) for y in range(6)]
    first += [(c, y, True) for c in range(2) for y in range(2, 4)]
    last = [(2, y, False) for y in range(6)] + [(2, y, True) for y in range(2, 4)]
    return first + last


def wrap_up(part, full_x, root, wrap, pressure, side, at_row, wave, back, grad, out, work):
    groups = 2 * part
    fixed = []
    for k in range(part):
        even, odd = pressure[2 * k], pressure[2 * k + 1]
        before = -0.5 * side(0, k, 1, 3)
        even = even + jnp.where(at_row == TOP - 1, 4.0 * before, 0.0)
        odd = odd + jnp.where(at_row == TOP + 8, 2.0 * side(1, k, 1, 0), 0.0)
        fixed.append((even, odd))
    near_low = [side(0, k, 0, 3) for k in range(part)]
    near_high = [side(1, k, 0, 0) for k in range(part)]
    pad = jnp.zeros((8 - 2 * part, WIDE), jnp.float32)
    edge_x = jnp.concatenate(near_low + near_high + [pad], axis=0)
    edge_slope = dot(edge_x, back[1], ((1,), (0,)))
    pressure = []
    for k in range(part):
        even, odd = fixed[k]
        scale = wave[k : k + 1, :]
        high = edge_slope[part + k : part + k + 1] + scale * side(1, k, 2, 0)
        high = high + 0.5 * side(1, k, 1, 1)
        low = edge_slope[k : k + 1] + scale * side(0, k, 2, 3) - 0.5 * side(0, k, 1, 2)
        pressure.append(even + jnp.where(at_row == TOP + 9, 4.0 * high, 0.0))
        pressure.append(odd + jnp.where(at_row == TOP - 2, 4.0 * low, 0.0))
    count = len(pressure)
    stacked = jnp.concatenate(pressure, axis=0)
    along = jnp.concatenate(wrap[:count], axis=0)
    size = count * SPAN
    work[0:size, :] = dot(along, back[0], ((1,), (0,))) - dot(stacked, grad[...], ((1,), (0,)))
    across = []
    upward = []
    for k in range(part):
        even, odd = pressure[2 * k], pressure[2 * k + 1]
        across.append(wrap[count + 2 * k] - 0.5 * (odd - pltpu.roll(odd, 1, 0)))
        across.append(wrap[count + 2 * k + 1] - 0.5 * (pltpu.roll(even, SPAN - 1, 0) - even))
        for j in range(2):
            upward.append(wrap[2 * count + 2 * k + j] + wave[k : k + 1, :] * pressure[2 * k + j])
    work[size : 3 * size, :] = dot(
        jnp.concatenate(across + upward, axis=0), back[0], ((1,), (0,))
    )
    slots = slot_of((8, 128))
    picks = slots_back()
    tiles = len(picks) // 4
    for s in range(8):
        for k in range(part):
            for tile_at in range(tiles):
                tile = None
                for v in range(4):
                    c, y, is_root = picks[4 * tile_at + v]
                    source = root if is_root else s
                    j, off = y % 2, y // 2 - 1
                    base = c * size + (2 * k + j) * SPAN + TOP + off
                    lanes = (source // 4) * 128
                    piece = work[base : base + 8, lanes : lanes + 128]
                    piece = moved_to(piece, source % 4, v)
                    tile = piece if tile is None else jnp.where(slots == v, piece, tile)
                row = s * 8 * part * tiles + k * tiles + tile_at
                out[pl.ds(row, 8, stride=part * tiles), :] = tile


def back_z(near, part, tiles, cosines, got, cos_rows, sin_rows, out):
    for tile in range(tiles):
        pieces = [got[pl.ds(k * tiles + tile, near, stride=part * tiles), :] for k in range(part)]
        table = cos_rows if tile < cosines else sin_rows
        block = dot(jnp.concatenate(pieces, axis=0), table[...], ((0,), (0,)))
        out[tile * 128 : (tile + 1) * 128, :] = block


def local(n_sec, split, velocity, prev_tendency, disk_cells, disk_kind, rotor_weights):
    slab, wide, depth = velocity.shape[1:]
    tx, tz, ty = split
    near, blocks, tiles = n_sec * ty, tx * tz, tx * tz * ty
    part = depth // near
    full_x = n_sec * slab
    sec_at = lax.axis_index("sec")
    near_at = lax.axis_index(NEAR)
    far_at = lax.axis_index(FAR)
    root = n_sec // 2 - 1
    fringe_slabs = (0, n_sec // 2, 3 * n_sec // 4, n_sec - 1)

    start = velocity.transpose(0, 2, 1, 3)
    low = lax.ppermute(start[:, :, -2:], "sec", ring(n_sec, 1))
    high = lax.ppermute(start[:, :, :2], "sec", ring(n_sec, -1))
    low, high, root_field = lax.optimization_barrier((low, high, start))
    extended = jnp.concatenate([low, start, high], axis=2)
    low = lax.ppermute(extended, TILE, ring(tiles, 1))
    high = lax.ppermute(extended, TILE, ring(tiles, -1))
    extended = jnp.concatenate([low, extended, high], axis=1)
    source = None
    for target in fringe_slabs:
        arrived = lax.ppermute(root_field, "sec", [(root, target)])
        source = arrived if source is None else source + arrived

    lam = fringe_rate * np.sin(np.pi * (np.arange(slab) + 0.5) / slab) ** 2
    flag = jnp.zeros((), jnp.float32)
    for target in fringe_slabs:
        flag = flag + (sec_at == target).astype(jnp.float32)
    lam_x = flag * f32(lam)[None, None, :, None]

    cells = slab * wide
    picked = disk_cells.reshape(-1)
    kinds = disk_kind.reshape(-1)
    weight = jnp.sum(
        jnp.where(kinds[:, None] == jnp.arange(KINDS)[None, :], rotor_weights[None, :], 0.0), axis=1
    )
    row_of = jnp.where(
        picked < cells * depth, (picked // depth % wide) * slab + picked // (depth * wide), cells
    )
    at_row = row_of[None, :] == jnp.arange(cells)[:, None]
    at_lane = (picked % depth)[:, None] == jnp.arange(depth)[None, :]
    drag = jnp.dot(
        jnp.where(at_row, weight[None, :], 0.0),
        at_lane.astype(jnp.float32),
        precision=precise,
    ).reshape(wide, slab, depth)

    cos_z, sin_z, cos_back, sin_back = z_tables(depth, near)
    plain_x, slope_x, make_back = x_tables(n_sec, slab)
    lines = line_tables(n_sec, slab, depth, ty, blocks, near_at, far_at)
    sides = jnp.stack([lax.rem(far_at + blocks - 1, blocks), lax.rem(far_at + 1, blocks)])
    turn = cas(np.arange(full_x), np.arange(full_x), full_x)
    turn_slope = 0.5 * (np.roll(turn, 1, axis=0) - np.roll(turn, -1, axis=0))
    edge_turn = np.zeros((WIDE, WIDE))
    edge_turn[:full_x, :full_x] = np.round(turn @ turn_slope / full_x, 12)

    def exchange(blocks_2d, count, axes):
        shaped = blocks_2d.reshape(count, -1, 128)
        got = lax.all_to_all(shaped, axes, split_axis=0, concat_axis=0, tiled=True)
        return got.reshape(-1, 128)

    def solve(interim, edges):
        groups = 2 * part
        height = 8 * groups
        (sent,) = kernel(
            functools.partial(forward_z, near, slab, part),
            [(near * groups, 128)],
            [(2 * 128, depth)] * 2,
            interim,
            cos_z,
            sin_z,
        )
        got = exchange(sent, near, NEAR)
        size = 4 * part + (12 * part if edges else 0)
        sent, modes, inner, ends = kernel(
            functools.partial(forward_x, part, edges, blocks),
            [(blocks * 2 * size, 128), (3 * height, WIDE), (height, WIDE), (groups, WIDE)],
            [(3 * height, WIDE), (size, WIDE)],
            got,
            plain_x,
            slope_x,
            lines["first"],
            lines["second"],
            lines["wave"],
        )
        got = exchange(sent, blocks, FAR)
        back, grad = make_back(2 if edges else 1)
        if edges:
            count = len(slots_back()) // 4
            operands = (
                sides,
                got,
                modes,
                inner,
                ends,
                lines["direct"],
                lines["spread"],
                lines["combine"],
                lines["wave"],
                jnp.stack([back, f32(edge_turn)]),
                grad,
            )
        else:
            count = 1
            operands = (
                got,
                inner,
                ends,
                lines["direct"],
                lines["spread"],
                lines["combine"],
                back,
            )
        (sent,) = kernel(
            functools.partial(back_x, part, edges, blocks, full_x, root),
            [(near * part * count, 128)],
            [((3 if edges else 1) * groups * SPAN, WIDE)],
            *operands,
            scalars=1 if edges else 0,
        )
        got = exchange(sent, near, NEAR)
        (cells_out,) = kernel(
            functools.partial(back_z, near, part, count, 4 if edges else 1),
            [(count * 128, depth)],
            [],
            got,
            cos_back,
            sin_back,
        )
        return cells_out.reshape(4 * count, 32, depth)

    tendency_old = prev_tendency.transpose(0, 2, 1, 3)
    for step_no in range(STEPS):
        current = extended[:, 2:-2, 2:-2]
        slopes = gradients(extended, -1.0)
        push = stress_force(strain_stress(slopes))
        inside = [slope[:, 1:-1, 1:-1] for slope in slopes]
        advect = current[0:1] * inside[0] + current[1:2] * inside[1] + current[2:3] * inside[2]
        fringe = lam_x * (source - current)
        turbine = -(drag * current[0] * jnp.abs(current[0]))
        empty = jnp.zeros_like(turbine)
        tendency = push - advect + jnp.stack([turbine, empty, empty]) + fringe
        interim = current + time_step * (1.5 * tendency - 0.5 * tendency_old)
        tendency_old = tendency
        if step_no < STEPS - 1:
            slots = solve(interim, True)
            fields = [slots[0:6], slots[6:12], slots[16:22]]
            extended = jnp.stack([field[:, : slab + 4] for field in fields])
            fields = [slots[12:14], slots[14:16], slots[22:24]]
            source = jnp.stack([field[:, 2 : slab + 2] for field in fields])
        else:
            pressure = solve(interim, False)[None, :, : slab + 2]
            current = interim - jnp.concatenate(gradients(pressure, 1.0), axis=0)
    return (current.transpose(0, 2, 1, 3), tendency.transpose(0, 2, 1, 3))


def solution(mesh):
    n_sec, tiles = mesh.shape["sec"], mesh.shape["tile"]
    split = SPLITS[tiles]
    fine = Mesh(mesh.devices.reshape((n_sec,) + split), ("sec",) + TILE)
    blocks = P(None, "sec", TILE, None)
    slots = P("sec", TILE, None)

    def body(*args):
        return local(n_sec, split, *args)

    return jax.shard_map(
        body,
        mesh=fine,
        in_specs=(blocks, blocks, slots, slots, P()),
        out_specs=(blocks, blocks),
        check_vma=False,
    )
```

```python
import functools
import math

import jax
import jax.numpy as jnp
import numpy as np
from jax import lax
from jax.experimental import pallas as pl
from jax.experimental.pallas import tpu as pltpu
from jax.sharding import Mesh
from jax.sharding import PartitionSpec as P

STEPS = 2
KINDS = 16
INTERPRET = False

precise = lax.Precision.HIGHEST
time_step = 0.1
fringe_rate = 2.0
smag_coef = 0.04

TILE = ("tx", "tz", "ty")
NEAR = ("sec", "ty")
FAR = ("tx", "tz")
SPLITS = {96: (4, 3, 8), 24: (1, 3, 8), 16: (2, 1, 8)}
WIDE = 256
SPAN = 24
TOP = 8
HALO = 2


def gradients(padded, z_sign):
    centre = padded[:, 1:-1, 1:-1, :]
    grad_x = 0.5 * (padded[:, 1:-1, 2:, :] - padded[:, 1:-1, :-2, :])
    grad_y = 0.5 * (padded[:, 2:, 1:-1, :] - padded[:, :-2, 1:-1, :])
    extended = jnp.concatenate(
        [z_sign * centre[..., :1], centre, z_sign * centre[..., -1:]], axis=-1
    )
    grad_z = 0.5 * (extended[..., 2:] - extended[..., :-2])
    return (grad_x, grad_y, grad_z)


def strain_stress(slopes):

    def strain(first, second):
        return 0.5 * (slopes[second][first] + slopes[first][second])

    strain_xx = strain(0, 0)
    strain_yy = strain(1, 1)
    strain_zz = strain(2, 2)
    strain_xy = strain(0, 1)
    strain_xz = strain(0, 2)
    strain_yz = strain(1, 2)
    squared = strain_xx * strain_xx + strain_yy * strain_yy + strain_zz * strain_zz
    squared = squared + 2.0 * (
        strain_xy * strain_xy + strain_xz * strain_xz + strain_yz * strain_yz
    )
    double = 2.0 * (smag_coef * jnp.sqrt(2.0 * squared + 0.01))
    return jnp.stack(
        [
            double * strain_xx,
            double * strain_yy,
            double * strain_zz,
            double * strain_xy,
            double * strain_xz,
            double * strain_yz,
        ]
    )


def stress_force(padded):
    grad_x, grad_y, grad_z = gradients(padded, 0.0)
    return jnp.stack(
        [
            grad_x[0] + grad_y[3] + grad_z[4],
            grad_x[3] + grad_y[1] + grad_z[5],
            grad_x[4] + grad_y[5] + grad_z[2],
        ]
    )


def ring(count, shift):
    return [(i, (i + shift) % count) for i in range(count)]


def swaps(count, first):
    pairs = [(t, (t + 1) % count) for t in range(first, count, 2)]
    return pairs + [(b, a) for a, b in pairs]


def f32(table):
    return jnp.asarray(np.asarray(table, np.float32))


def cas(rows, cols, length):
    angle = 2.0 * np.pi * ((np.asarray(rows)[:, None] * np.asarray(cols)[None, :]) % length)
    angle = angle / length
    return np.cos(angle) + np.sin(angle)


def lane_modes(full_x):
    modes = np.zeros(WIDE, np.int64)
    modes[:full_x] = np.arange(full_x)
    modes[full_x + 1] = full_x // 2
    return modes


def z_tables(depth, near):
    points = np.arange(depth) + 0.5
    modes = np.arange(depth)
    cosine = np.cos(np.pi * modes[:, None] * points[None, :] / depth)
    sine = np.sin(np.pi * modes[:, None] * points[None, :] / depth)
    sine[0] = (-1.0) ** np.arange(depth)
    weight = np.sqrt(np.where(modes == 0, 1.0 / depth, 2.0 / depth))[:, None]
    part = depth // near

    def order(table):
        table = (table * weight).reshape(near, part, depth).transpose(1, 0, 2)
        return f32(table.reshape(depth, depth))

    return order(cosine), order(sine)


def x_tables(n_sec, slab):
    full_x = n_sec * slab
    at = ((np.arange(n_sec) * slab)[:, None] + np.arange(32) - HALO).reshape(-1)
    table = cas(at % full_x, lane_modes(full_x), full_x) / np.sqrt(full_x)
    table[:, full_x + 2 :] = 0.0
    modes = np.arange(full_x)
    slope = np.zeros((WIDE, WIDE))
    slope[(-modes) % full_x, modes] = -np.sin(2.0 * np.pi * modes / full_x)
    slope[0, 0] = 0.0
    slope[full_x // 2, full_x // 2] = 0.0
    return f32(table), f32(slope)


def line_tables(n_sec, slab, depth, size, blocks, near_at, far_at):
    full_x = n_sec * slab
    count = size * blocks
    near = n_sec * size
    part = depth // near
    modes = lane_modes(full_x)
    wave_x = np.sin(2.0 * np.pi * modes / full_x) ** 2
    wave_x[modes % (full_x // 2) == 0] = 0.0
    wave_z = np.sin(np.pi * np.arange(depth) / depth) ** 2
    level = lax.dynamic_slice_in_dim(f32(wave_z), near_at * part, part)
    both = level[:, None] + f32(wave_x)[None, :]
    tall = jnp.sqrt(1.0 + both)
    mu = 2.0 * jnp.log1p(jnp.sqrt(both) + both / (1.0 + tall))
    flat = both == 0.0
    lane_at = jnp.arange(WIDE)
    twin = flat & (lane_at >= full_x)[None, :]
    safe = jnp.where(flat, 1.0, jnp.sqrt(both) * tall * (1.0 - jnp.exp(-count * mu)))
    gain = jnp.where(flat, 0.0, 1.0 / safe)
    real = (lane_at < full_x).astype(jnp.float32)

    def decay(distance):
        return jnp.exp(-distance * mu_of(distance))

    def mu_of(distance):
        return mu.reshape((part,) + (1,) * (distance.ndim - 2) + (WIDE,))

    def lanes(table, like):
        return table.reshape((part,) + (1,) * (like.ndim - 2) + (WIDE,))

    def grid(values):
        values = jnp.asarray(values, jnp.float32)
        return jnp.broadcast_to(values[None, ..., None], (part,) + values.shape + (1,))

    def pick(plain, special, like):
        return jnp.where(lanes(flat, like), special, plain)

    index = grid(np.arange(-1, size + 1))
    second = jnp.where(lanes(twin, index), index * index, jnp.ones_like(index))
    first_w = pick(decay(index), second, index)
    second_w = pick(decay(size - 1 - index), index, index)
    second_w = jnp.where(lanes(twin, index), 0.0, second_w)

    def green(distance):
        plain = -lanes(gain, distance) * (decay(distance) + decay(count - distance))
        special = 2.0 * distance * (count - distance) / count - (count**2 - 1) / (3.0 * count)
        return pick(plain, special, distance)

    cells = np.arange(SPAN) - TOP
    valid = ((cells >= -2) & (cells <= size + 1)).astype(np.float32)
    keep = grid(valid)
    sources = np.concatenate([np.arange(size), [-1, size]])
    direct = green(grid(np.abs(cells[None, :] - sources[:, None]))) * (keep[:, None] * real)
    spot = grid(cells)
    keep = keep * real
    from_low = pick(-lanes(gain, spot) * decay(spot), 1.0, spot) * keep
    from_high = pick(-lanes(gain, spot) * decay(size - 1 - spot), spot, spot) * keep
    square = pick(0.0, -2.0 * spot * spot / count, spot) * keep
    shift = pick(0.0, -2.0 / count + 0.0 * spot, spot) * keep

    step = lax.rem(far_at - jnp.arange(blocks) + blocks, blocks).astype(jnp.float32)
    away = jnp.broadcast_to(step[None, :, None], (part, blocks, 1))
    other = away > 0.5
    jump = size * away
    low_two = pick(decay(jump - (size - 1)), 2.0 * (2.0 * jump - count) / count, jump)
    low_one = pick(
        0.0,
        2.0 * jump * (count - jump) / count - (count**2 - 1) / (3.0 * count),
        jump,
    )
    high_one = pick(decay(count - (size - 1) - jump), 2.0 * (count - 2.0 * jump) / count, jump)
    high_two = pick(0.0, 4.0 / count + 0.0 * jump, jump)
    whole = jnp.ones_like(low_two)

    def rows(one, two):
        pair = jnp.stack([jnp.broadcast_to(one, low_two.shape), jnp.broadcast_to(two, low_two.shape)], 2)
        pair = jnp.where(other[..., None], pair, 0.0)
        pair = jnp.broadcast_to(pair[:, :, None], (part, blocks, 2, 2, WIDE))
        return pair.transpose(1, 0, 2, 3, 4).reshape(blocks, part * 4, WIDE)

    combine = jnp.stack([rows(low_one, low_two), rows(high_one, high_two), rows(whole, 0.0 * whole)])
    spread = jnp.stack([from_low, from_high, square, shift])
    wave = lax.dynamic_slice_in_dim(
        f32(np.sin(np.pi * np.arange(depth) / depth)), near_at * part, part
    )
    wave = jnp.broadcast_to(wave[:, None], (part, WIDE))
    return dict(first=first_w, second=second_w, direct=direct, spread=spread, combine=combine, wave=wave)


def dot(left, right, contract):
    return lax.dot_general(
        left, right, (contract, ((), ())), precision=precise, preferred_element_type=jnp.float32
    )


def kernel(body, out_shapes, scratch, *operands, scalars=0):
    spaces = [pl.BlockSpec(memory_space=pltpu.SMEM)] * scalars
    spaces += [pl.BlockSpec(memory_space=pltpu.VMEM)] * (len(operands) - scalars)
    shapes = [jax.ShapeDtypeStruct(shape, jnp.float32) for shape in out_shapes]
    moved = sum(4 * math.prod(item.shape) for item in list(operands) + shapes)
    return pl.pallas_call(
        body,
        out_shape=shapes,
        in_specs=spaces,
        out_specs=[pl.BlockSpec(memory_space=pltpu.VMEM)] * len(shapes),
        scratch_shapes=[pltpu.VMEM(shape, jnp.float32) for shape in scratch],
        cost_estimate=pl.CostEstimate(flops=10**7, bytes_accessed=moved, transcendentals=0),
        compiler_params=pltpu.CompilerParams(vmem_limit_bytes=24 * 2**20),
        interpret=pltpu.InterpretParams() if INTERPRET else False,
    )(*operands)


def forward_z(near, slab, part, field, cos_rows, sin_rows, out, even, odd):
    even[...] = jnp.zeros_like(even)
    odd[...] = jnp.zeros_like(odd)
    for j in range(2):
        for c in range(3):
            kept = even if c < 2 else odd
            first = j * 128 + c * 32 + HALO
            kept[first : first + slab, :] = field[c, j]
    result = dot(cos_rows[...], even[...], ((1,), (1,)))
    result = result + dot(sin_rows[...], odd[...], ((1,), (1,)))
    for k in range(part):
        for j in range(2):
            piece = result[k * near : (k + 1) * near, j * 128 : (j + 1) * 128]
            out[pl.ds(k * 2 + j, near, stride=2 * part), :] = piece


def slot_of(shape):
    return lax.broadcasted_iota(jnp.int32, shape, 1) // 32


def moved_to(piece, source, target):
    shift = (32 * (target - source)) % 128
    return piece if shift == 0 else pltpu.roll(piece, shift, 1)


def forward_x(
    part, edges, blocks, got, plain, slope, first, second, wave, out, modes, inner, ends, lhs, rows
):
    slots = slot_of((8, 128))
    groups = 2 * part
    for t in range(2):
        for g in range(groups):
            for c in range(3):
                total = None
                for u in range(4):
                    s = 4 * t + u
                    piece = got[pl.ds(s * 8 * groups + g, 8, stride=groups), :]
                    piece = moved_to(piece, c, u)
                    total = piece if total is None else jnp.where(slots == u, piece, total)
                base = c * 8 * groups + g * 8
                lhs[base : base + 8, t * 128 : (t + 1) * 128] = total
    height = 8 * groups
    fields = dot(lhs[...], plain[...], ((1,), (0,)))
    modes[...] = fields
    sloped = dot(fields[0:height], slope[...], ((1,), (0,)))
    at_row = lax.broadcasted_iota(jnp.int32, (8, WIDE), 0)
    for k in range(part):
        sources = []
        crossing = []
        for j in range(2):
            base = (2 * k + j) * 8
            vertical = modes[2 * height + base : 2 * height + base + 8, :]
            sources.append(sloped[base : base + 8] + wave[k : k + 1, :] * vertical)
            crossing.append(modes[height + base : height + base + 8, :])
        below = jnp.where(at_row == 0, 0.0, pltpu.roll(crossing[1], 1, 0))
        above = jnp.where(at_row == 7, 0.0, pltpu.roll(crossing[0], 7, 0))
        lines = [
            sources[0] + 0.5 * (crossing[1] - below),
            sources[1] + 0.5 * (above - crossing[0]),
        ]
        outside = [-0.5 * crossing[1][7:8, :], 0.5 * crossing[0][0:1, :]]
        for j in range(2):
            base = (2 * k + j) * 8
            inner[base : base + 8, :] = lines[j]
            ends[2 * k + j : 2 * k + j + 1, :] = outside[j]
            past = 9 if j == 0 else 0
            for r, table in enumerate((first, second)):
                moment = jnp.sum(table[k, 1:9, :] * lines[j], axis=0, keepdims=True)
                moment = moment + table[k, past : past + 1, :] * outside[j]
                at = k * 4 + j * 2 + r
                rows[at : at + 1, :] = moment
    if edges:
        for k in range(part):
            for c in range(3):
                for e in range(4):
                    source = c * height + (2 * k + e % 2) * 8 + (0 if e < 2 else 7)
                    at = 4 * part + k * 12 + c * 4 + e
                    rows[at : at + 1, :] = modes[source : source + 1, :]
    size = rows.shape[0]
    for h in range(2):
        half = rows[:, h * 128 : (h + 1) * 128]
        for n in range(blocks):
            out[(n * 2 + h) * size : (n * 2 + h + 1) * size, :] = half


def back_x(
    part, edges, blocks, full_x, root, *refs
):
    if edges:
        (sides, got, modes, inner, ends, direct, spread, combine, wave, back, slope, out, work) = refs
    else:
        (got, inner, ends, direct, spread, combine, back, out, work) = refs
    size = got.shape[0] // (2 * blocks)
    groups = 2 * part
    height = 8 * groups
    lane = lax.broadcasted_iota(jnp.int32, (1, WIDE), 1)
    sums = []
    for r in range(3):
        halves = []
        for h in range(2):
            total = None
            for n in range(blocks):
                piece = got[(n * 2 + h) * size : (n * 2 + h) * size + 4 * part, :]
                piece = combine[r, n, :, h * 128 : (h + 1) * 128] * piece
                total = piece if total is None else total + piece
            halves.append(total)
        sums.append(jnp.concatenate(halves, axis=1))
    side_rows = []
    if edges:
        for which in range(2):
            halves = []
            for h in range(2):
                start = pl.multiple_of((sides[which] * 2 + h) * size + 4 * part, 8)
                halves.append(got[pl.ds(start, 12 * part), :])
            side_rows.append(jnp.concatenate(halves, axis=1))

    def side(which, k, c, e):
        at = k * 12 + c * 4 + e
        return side_rows[which][at : at + 1, :]

    at_row = lax.broadcasted_iota(jnp.int32, (SPAN, WIDE), 0)
    row8 = lax.broadcasted_iota(jnp.int32, (8, WIDE), 0)
    pressure = []
    for k in range(part):
        for j in range(2):
            g = 2 * k + j
            line = inner[g * 8 : g * 8 + 8, :]
            total = None
            for i in range(8):
                term = direct[k, i] * line[i : i + 1, :]
                total = term if total is None else total + term
            total = total + direct[k, 9 if j == 0 else 8] * ends[g : g + 1, :]
            for r in range(3):
                one = sums[r][2 * g : 2 * g + 1, :] + sums[r][2 * g + 1 : 2 * g + 2, :]
                total = total + spread[r, k] * one
                if r == 2:
                    far = jnp.where(
                        lane == 0,
                        one[:, full_x : full_x + 1],
                        jnp.where(lane == full_x // 2, one[:, full_x + 1 : full_x + 2], 0.0),
                    )
                    total = total + spread[3, k] * far
            pressure.append(total)
    if edges:
        wrap = []
        for c in range(3):
            for k in range(part):
                for j in range(2):
                    g = 2 * k + j
                    own = modes[c * height + g * 8 : c * height + g * 8 + 8, :]
                    low = jnp.where(row8 == 7, side(0, k, c, 2 + j), 0.0)
                    high = jnp.where(row8 == 0, side(1, k, c, j), 0.0)
                    wrap.append(jnp.concatenate([low, own, high], axis=0))
        return wrap_up(
            part, full_x, root, wrap, pressure, side, at_row, wave, back, slope, out, work
        )
    work[...] = dot(jnp.concatenate(pressure, axis=0), back[...], ((1,), (1,)))
    slots = slot_of((8, 128))
    picks = ((1, -1), (0, 0), (1, 0), (0, 1))
    for s in range(8):
        for k in range(part):
            tile = None
            for v, (j, off) in enumerate(picks):
                base = (2 * k + j) * SPAN + TOP + off
                piece = work[base : base + 8, (s // 4) * 128 : (s // 4) * 128 + 128]
                piece = moved_to(piece, s % 4, v)
                tile = piece if tile is None else jnp.where(slots == v, piece, tile)
            out[pl.ds(s * 8 * part + k, 8, stride=part), :] = tile


def slots_back():
    first = [(c, y, False) for c in range(2) for y in range(6)]
    first += [(c, y, True) for c in range(2) for y in range(2, 4)]
    last = [(2, y, False) for y in range(6)] + [(2, y, True) for y in range(2, 4)]
    return first + last


def wrap_up(part, full_x, root, wrap, pressure, side, at_row, wave, back, slope, out, work):
    groups = 2 * part
    fixed = []
    for k in range(part):
        even, odd = pressure[2 * k], pressure[2 * k + 1]
        before = -0.5 * side(0, k, 1, 3)
        even = even + jnp.where(at_row == TOP - 1, 4.0 * before, 0.0)
        odd = odd + jnp.where(at_row == TOP + 8, 2.0 * side(1, k, 1, 0), 0.0)
        fixed.append((even, odd))
    near_low = [side(0, k, 0, 3) for k in range(part)]
    near_high = [side(1, k, 0, 0) for k in range(part)]
    pad = jnp.zeros((8 - 2 * part, WIDE), jnp.float32)
    edge_x = jnp.concatenate(near_low + near_high + [pad], axis=0)
    edge_slope = dot(edge_x, slope[...], ((1,), (0,)))
    pressure = []
    for k in range(part):
        even, odd = fixed[k]
        scale = wave[k : k + 1, :]
        high = edge_slope[part + k : part + k + 1] + scale * side(1, k, 2, 0)
        high = high + 0.5 * side(1, k, 1, 1)
        low = edge_slope[k : k + 1] + scale * side(0, k, 2, 3) - 0.5 * side(0, k, 1, 2)
        pressure.append(even + jnp.where(at_row == TOP + 9, 4.0 * high, 0.0))
        pressure.append(odd + jnp.where(at_row == TOP - 2, 4.0 * low, 0.0))
    count = len(pressure)
    stacked = jnp.concatenate(pressure, axis=0)
    along = jnp.concatenate(wrap[:count], axis=0) - dot(stacked, slope[...], ((1,), (0,)))
    size = count * SPAN
    across = []
    upward = []
    for k in range(part):
        even, odd = pressure[2 * k], pressure[2 * k + 1]
        across.append(wrap[count + 2 * k] - 0.5 * (odd - pltpu.roll(odd, 1, 0)))
        across.append(wrap[count + 2 * k + 1] - 0.5 * (pltpu.roll(even, SPAN - 1, 0) - even))
        for j in range(2):
            upward.append(wrap[2 * count + 2 * k + j] + wave[k : k + 1, :] * pressure[2 * k + j])
    fields = jnp.concatenate([along] + across + upward, axis=0)
    lanes = lax.broadcasted_iota(jnp.int32, fields.shape, 1)
    fields = jnp.where(lanes < full_x, fields, 0.0)
    work[...] = dot(fields, back[...], ((1,), (1,)))
    slots = slot_of((8, 128))
    picks = slots_back()
    tiles = len(picks) // 4
    for s in range(8):
        for k in range(part):
            for tile_at in range(tiles):
                tile = None
                for v in range(4):
                    c, y, is_root = picks[4 * tile_at + v]
                    source = root if is_root else s
                    j, off = y % 2, y // 2 - 1
                    base = c * size + (2 * k + j) * SPAN + TOP + off
                    lanes = (source // 4) * 128
                    piece = work[base : base + 8, lanes : lanes + 128]
                    piece = moved_to(piece, source % 4, v)
                    tile = piece if tile is None else jnp.where(slots == v, piece, tile)
                row = s * 8 * part * tiles + k * tiles + tile_at
                out[pl.ds(row, 8, stride=part * tiles), :] = tile


def back_z(near, part, tiles, cosines, got, cos_rows, sin_rows, out):
    for tile in range(tiles):
        pieces = [got[pl.ds(k * tiles + tile, near, stride=part * tiles), :] for k in range(part)]
        table = cos_rows if tile < cosines else sin_rows
        block = dot(jnp.concatenate(pieces, axis=0), table[...], ((0,), (0,)))
        out[tile * 128 : (tile + 1) * 128, :] = block


def local(n_sec, split, velocity, prev_tendency, disk_cells, disk_kind, rotor_weights):
    slab, wide, depth = velocity.shape[1:]
    tx, tz, ty = split
    near, blocks, tiles = n_sec * ty, tx * tz, tx * tz * ty
    part = depth // near
    full_x = n_sec * slab
    sec_at = lax.axis_index("sec")
    near_at = lax.axis_index(NEAR)
    far_at = lax.axis_index(FAR)
    root = n_sec // 2 - 1
    fringe_slabs = (0, n_sec // 2, 3 * n_sec // 4, n_sec - 1)

    start = velocity.transpose(0, 2, 1, 3)
    low = lax.ppermute(start[:, :, -2:], "sec", ring(n_sec, 1))
    high = lax.ppermute(start[:, :, :2], "sec", ring(n_sec, -1))
    extended = jnp.concatenate([low, start, high], axis=2)
    (extended, root_field, sec_at, near_at, far_at, disk_cells, disk_kind) = (
        lax.optimization_barrier(
            (extended, start, sec_at, near_at, far_at, disk_cells, disk_kind)
        )
    )
    far_swap = lax.ppermute(extended, TILE, swaps(tiles, 1))
    near_swap = lax.ppermute(extended, TILE, swaps(tiles, 0))
    is_even = lax.axis_index("ty") % 2 == 0
    low = jnp.where(is_even, far_swap, near_swap)
    high = jnp.where(is_even, near_swap, far_swap)
    extended = jnp.concatenate([low, extended, high], axis=1)
    lam = fringe_rate * np.sin(np.pi * (np.arange(slab) + 0.5) / slab) ** 2
    flag = jnp.zeros((), jnp.float32)
    for target in fringe_slabs:
        flag = flag + (sec_at == target).astype(jnp.float32)
    lam_x = flag * f32(lam)[None, None, :, None]

    cells = slab * wide
    picked = disk_cells.reshape(-1)
    kinds = disk_kind.reshape(-1)
    weight = jnp.sum(
        jnp.where(kinds[:, None] == jnp.arange(KINDS)[None, :], rotor_weights[None, :], 0.0), axis=1
    )
    row_of = jnp.where(
        picked < cells * depth, (picked // depth % wide) * slab + picked // (depth * wide), cells
    )
    at_row = row_of[None, :] == jnp.arange(cells)[:, None]
    at_lane = (picked % depth)[:, None] == jnp.arange(depth)[None, :]
    drag = jnp.dot(
        jnp.where(at_row, weight[None, :], 0.0),
        at_lane.astype(jnp.float32),
        precision=precise,
    ).reshape(wide, slab, depth)

    root_field, drag = lax.optimization_barrier((root_field, drag))
    source = None
    for target in fringe_slabs:
        arrived = lax.ppermute(root_field, "sec", [(root, target)])
        source = arrived if source is None else source + arrived

    cos_z, sin_z = z_tables(depth, near)
    table_x, slope_x = x_tables(n_sec, slab)
    lines = line_tables(n_sec, slab, depth, ty, blocks, near_at, far_at)
    sides = jnp.stack([lax.rem(far_at + blocks - 1, blocks), lax.rem(far_at + 1, blocks)])

    def exchange(blocks_2d, count, axes):
        shaped = blocks_2d.reshape(count, -1, 128)
        got = lax.all_to_all(shaped, axes, split_axis=0, concat_axis=0, tiled=True)
        return got.reshape(-1, 128)

    def solve(interim, edges):
        groups = 2 * part
        height = 8 * groups
        (sent,) = kernel(
            functools.partial(forward_z, near, slab, part),
            [(near * groups, 128)],
            [(2 * 128, depth)] * 2,
            interim,
            cos_z,
            sin_z,
        )
        got = exchange(sent, near, NEAR)
        size = 4 * part + (12 * part if edges else 0)
        sent, modes, inner, ends = kernel(
            functools.partial(forward_x, part, edges, blocks),
            [(blocks * 2 * size, 128), (3 * height, WIDE), (height, WIDE), (groups, WIDE)],
            [(3 * height, WIDE), (size, WIDE)],
            got,
            table_x,
            slope_x,
            lines["first"],
            lines["second"],
            lines["wave"],
        )
        got = exchange(sent, blocks, FAR)
        if edges:
            count = len(slots_back()) // 4
            operands = (
                sides,
                got,
                modes,
                inner,
                ends,
                lines["direct"],
                lines["spread"],
                lines["combine"],
                lines["wave"],
                table_x,
                slope_x,
            )
        else:
            count = 1
            operands = (
                got,
                inner,
                ends,
                lines["direct"],
                lines["spread"],
                lines["combine"],
                table_x,
            )
        (sent,) = kernel(
            functools.partial(back_x, part, edges, blocks, full_x, root),
            [(near * part * count, 128)],
            [((3 if edges else 1) * groups * SPAN, WIDE)],
            *operands,
            scalars=1 if edges else 0,
        )
        got = exchange(sent, near, NEAR)
        (cells_out,) = kernel(
            functools.partial(back_z, near, part, count, 4 if edges else 1),
            [(count * 128, depth)],
            [],
            got,
            cos_z,
            sin_z,
        )
        return cells_out.reshape(4 * count, 32, depth)

    tendency_old = prev_tendency.transpose(0, 2, 1, 3)
    for step_no in range(STEPS):
        current = extended[:, 2:-2, 2:-2]
        slopes = gradients(extended, -1.0)
        push = stress_force(strain_stress(slopes))
        inside = [slope[:, 1:-1, 1:-1] for slope in slopes]
        advect = current[0:1] * inside[0] + current[1:2] * inside[1] + current[2:3] * inside[2]
        fringe = lam_x * (source - current)
        turbine = -(drag * current[0] * jnp.abs(current[0]))
        empty = jnp.zeros_like(turbine)
        tendency = push - advect + jnp.stack([turbine, empty, empty]) + fringe
        interim = current + time_step * (1.5 * tendency - 0.5 * tendency_old)
        tendency_old = tendency
        if step_no < STEPS - 1:
            slots = solve(interim, True)
            fields = [slots[0:6], slots[6:12], slots[16:22]]
            extended = jnp.stack([field[:, : slab + 4] for field in fields])
            fields = [slots[12:14], slots[14:16], slots[22:24]]
            source = jnp.stack([field[:, 2 : slab + 2] for field in fields])
        else:
            pressure = solve(interim, False)[None, :, 1 : slab + 3]
            current = interim - jnp.concatenate(gradients(pressure, 1.0), axis=0)
    return (current.transpose(0, 2, 1, 3), tendency.transpose(0, 2, 1, 3))


def solution(mesh):
    n_sec, tiles = mesh.shape["sec"], mesh.shape["tile"]
    split = SPLITS[tiles]
    fine = Mesh(mesh.devices.reshape((n_sec,) + split), ("sec",) + TILE)
    blocks = P(None, "sec", TILE, None)
    slots = P("sec", TILE, None)

    def body(*args):
        return local(n_sec, split, *args)

    return jax.shard_map(
        body,
        mesh=fine,
        in_specs=(blocks, blocks, slots, slots, P()),
        out_specs=(blocks, blocks),
        check_vma=False,
    )
```
